256 devices in a mesh: win: 32 (over z_hi, y, core), chan: 8 (over z_lo, x).
Axes of the slice: x: 4, y: 4, z: 8 (z_hi: 4, z_lo: 2; z = z_hi * 2 + z_lo), core: 2. Of those that a mesh axis runs over, the one named last changes fastest.
Arguments:
- traces: bfloat16 [64, 2048, 4096], P('win', 'chan'), may hold values from -120 to 120
- block_pairs: int32 [32, 2], replicated, may hold values from 0 to 15
- valid_count: int32 [1], replicated, may hold values from 8 to 31
Outputs:
- cross_spectra: float32 [32, 8, 2, 128, 128], P('win', 'chan')
The draws below stay inside these ranges and needn't reach their ends.
Inputs may be any that keep to these rules, and one draw needn't show every extreme that they name: `block_pairs`: entries are channel block numbers; a pair may repeat.
All inputs are finite; a program needn't handle non-finite values.
Results may differ from the reference program's by a relative error of at most 0.0037.
Values may be sent and summed in bfloat16 or wider, within the bound.
No kernel may reach another device: no remote copies, remote signals or barrier semaphores. Data moves between devices by JAX's collectives and lax.ppermute only.
A program may use at most 64 MiB of HBM per device.

```python
import math
import jax
import jax.numpy as jnp
from jax import lax

NT = 4096
BLOCK = 128
NBINS = 256
FREQ_LO = 64
GROUP = 32
WINDOWS = 64
CH = 2048
NB = 16
NP = 32
GROUPS = 8


def draw_traces(key, part):
    keys = jax.random.split(jax.random.fold_in(key, 7), 5)
    noise = jnp.clip(jax.random.normal(keys[0], (WINDOWS, CH, NT), jnp.float32), -6.0, 6.0)
    gain = jnp.exp(jax.random.uniform(keys[1], (1, CH, 1), jnp.float32, 0.0, math.log(10.0)))
    tone_bin = FREQ_LO + jax.random.randint(keys[2], (1, CH, 1), 0, NBINS)
    amplitude = jnp.exp(jax.random.uniform(keys[3], (1, CH, 1), jnp.float32, math.log(0.1), math.log(0.5)))
    phase = jax.random.uniform(keys[4], (WINDOWS, CH, 1), jnp.float32, -math.pi, math.pi)
    times = jnp.arange(NT, dtype=jnp.int32)[None, None, :]
    turns = times * tone_bin % NT
    tone = amplitude * jnp.cos(turns.astype(jnp.float32) * (2.0 * math.pi / NT) + phase)
    return (gain * (noise + tone)).astype(jnp.bfloat16)


def with_ends(entries, key, least, high):
    dims = entries.shape
    spot = [jax.random.randint(jax.random.fold_in(key, axis), (), 0, dims[axis]) for axis in range(len(dims))]
    entries = entries.at[tuple(spot)].set(least)
    longest = dims.index(max(dims))
    spot[longest] = (spot[longest] + 1) % dims[longest]
    return entries.at[tuple(spot)].set(high)


def setup_inputs(seed: int = 0) -> dict:
    seeds = jax.random.split(jax.random.key(seed), 4)
    return {
        "traces": draw_traces(jax.random.fold_in(seeds[3], 71), 0),
        "block_pairs": with_ends(jax.random.randint(seeds[1], (NP, 2), 0, NB), jax.random.fold_in(seeds[1], 1), 0, NB - 1).astype(jnp.int32),
        "valid_count": jax.random.randint(seeds[2], (1,), NP // 4, NP).astype(jnp.int32),
    }


def dft_table(length, first_bin, bins):
    times = jnp.arange(length, dtype=jnp.int32)
    freqs = first_bin + jnp.arange(bins, dtype=jnp.int32)
    phases = times[:, None] * freqs[None, :] % length
    angles = phases.astype(jnp.float32) * (2.0 * math.pi / length)
    factor = 1.0 / math.sqrt(length)
    return (jnp.concatenate([jnp.cos(angles), -jnp.sin(angles)], axis=1) * factor).astype(jnp.bfloat16)

def reference(traces, block_pairs, valid_count):
    table = dft_table(NT, FREQ_LO, NBINS)

    def whiten(window_traces):
        spectra = jnp.dot(window_traces, table, preferred_element_type=jnp.float32)
        energy = lax.optimization_barrier(jnp.sum(spectra * spectra, axis=1, keepdims=True)) / NBINS
        return (spectra * lax.rsqrt(energy + 1e-06)).astype(jnp.bfloat16)
    whitened = lax.map(whiten, traces)
    real_part = whitened[:, :, :NBINS].astype(jnp.float32).reshape(WINDOWS, CH, GROUPS, GROUP)
    imag_part = whitened[:, :, NBINS:].astype(jnp.float32).reshape(WINDOWS, CH, GROUPS, GROUP)
    stack_scale = 1.0 / math.sqrt(WINDOWS * GROUP)
    high = lax.Precision.HIGHEST

    def one_slot(slot):
        row_start = (block_pairs[slot, 0] * BLOCK).astype(jnp.int32)
        col_start = (block_pairs[slot, 1] * BLOCK).astype(jnp.int32)
        a_re = lax.dynamic_slice_in_dim(real_part, row_start, BLOCK, 1)
        a_im = lax.dynamic_slice_in_dim(imag_part, row_start, BLOCK, 1)
        b_re = lax.dynamic_slice_in_dim(real_part, col_start, BLOCK, 1)
        b_im = lax.dynamic_slice_in_dim(imag_part, col_start, BLOCK, 1)
        sum_re = jnp.einsum('wigf,wjgf->gij', a_re, b_re, precision=high) + jnp.einsum('wigf,wjgf->gij', a_im, b_im, precision=high)
        sum_im = jnp.einsum('wigf,wjgf->gij', a_im, b_re, precision=high) - jnp.einsum('wigf,wjgf->gij', a_re, b_im, precision=high)
        live = (slot < valid_count[0]).astype(jnp.float32)
        return jnp.stack([sum_re, sum_im], axis=1) * (stack_scale * live)
    return lax.map(one_slot, jnp.arange(NP, dtype=jnp.int32))
```

```python
import math

import jax
import jax.numpy as jnp
import numpy as np
from jax import lax
from jax.experimental import pallas as pl
from jax.experimental.pallas import tpu as pltpu
from jax.sharding import Mesh, PartitionSpec as P

BLOCK = 128
NBINS = 256
FREQ_LO = 64
GROUP = 32
EPS = 1e-06
QUARTERS = 4


def packed_table(length):
    times = np.arange(length // QUARTERS, dtype=np.int64)
    freqs = FREQ_LO + np.arange(NBINS, dtype=np.int64)
    angles = (times[:, None] * freqs[None, :] % length) * (2.0 * math.pi / length)
    factor = 1.0 / math.sqrt(length)
    re = (np.cos(angles) * factor).reshape(-1, NBINS // 64, 64)
    im = (-np.sin(angles) * factor).reshape(-1, NBINS // 64, 64)
    return np.concatenate([re, im], axis=2).reshape(-1, 2 * NBINS).astype(jnp.bfloat16)


def spectra_kernel(traces, table, out, table_buf, buf, sems):
    steps, windows, span, length = buf.shape
    quarter = length // QUARTERS
    load_table = pltpu.make_async_copy(table, table_buf, sems.at[steps])
    load_table.start()
    loads = []
    for step in range(steps):
        load = pltpu.make_async_copy(
            traces.at[:, pl.ds(step * span, span), :], buf.at[step], sems.at[step]
        )
        load.start()
        loads.append(load)
    lanes = lax.broadcasted_iota(jnp.int32, (span, 128), 1)
    bin4 = (FREQ_LO + lanes) % 4
    sign2 = jnp.where(bin4 % 2 == 0, 1.0, -1.0)
    direct = jnp.where(bin4 == 0, 1.0, jnp.where(bin4 == 2, -1.0, 0.0))
    up = jnp.where(bin4 == 1, 1.0, jnp.where(bin4 == 3, -1.0, 0.0))
    cross = jnp.where(lanes < 64, up, -up)
    lane32 = lanes // 32 % 2
    tiles = 2 * NBINS // 128
    load_table.wait()
    for step in range(steps):
        loads[step].wait()
        whole = buf[step].reshape(windows * span, length)
        stacked = jnp.concatenate(
            [whole[:, q * quarter : (q + 1) * quarter] for q in range(QUARTERS)], axis=0
        )
        dots = jnp.dot(stacked, table_buf[...], preferred_element_type=jnp.float32)
        spans = []
        for w in range(windows):
            parts = []
            energy = jnp.zeros((span, 1), jnp.float32)
            for t in range(tiles):
                cols = slice(t * 128, (t + 1) * 128)
                d0, d1, d2, d3 = (
                    dots[(q * windows + w) * span : (q * windows + w + 1) * span, cols]
                    for q in range(QUARTERS)
                )
                main = d0 + sign2 * d2
                turn = d1 + sign2 * d3
                full = main + direct * turn + cross * pltpu.roll(turn, 64, 1)
                energy = energy + jnp.sum(full * full, axis=1, keepdims=True)
                parts.append(full)
            scale = lax.rsqrt(energy / NBINS + EPS)
            spans.append([part * scale for part in parts])
        rows = pl.ds(step * span, span)
        for t in range(tiles):
            first, second = spans[0][t], spans[1][t]
            out[2 * t, rows] = jnp.where(lane32 == 0, first, pltpu.roll(second, 32, 1)).astype(out.dtype)
            out[2 * t + 1, rows] = jnp.where(lane32 == 1, first, pltpu.roll(second, 96, 1)).astype(
                out.dtype
            )


def whitened_groups(traces, steps=4):
    windows, channels, length = traces.shape
    table = jnp.asarray(packed_table(length))
    groups = NBINS // GROUP
    return pl.pallas_call(
        spectra_kernel,
        out_shape=jax.ShapeDtypeStruct((groups, channels, windows * 2 * GROUP), jnp.bfloat16),
        in_specs=[pl.BlockSpec(memory_space=pltpu.HBM), pl.BlockSpec(memory_space=pltpu.HBM)],
        out_specs=pl.BlockSpec(memory_space=pltpu.VMEM),
        scratch_shapes=[
            pltpu.VMEM(table.shape, table.dtype),
            pltpu.VMEM((steps, windows, channels // steps, length), traces.dtype),
            pltpu.SemaphoreType.DMA((steps + 1,)),
        ],
        compiler_params=pltpu.CompilerParams(vmem_limit_bytes=48 << 20),
        name="spectra",
    )(pltpu.with_memory_space_constraint(traces, pltpu.HBM), pltpu.with_memory_space_constraint(table, pltpu.HBM))


def products_kernel(pairs, own, sib, out):
    lanes = lax.broadcasted_iota(jnp.int32, (BLOCK, 128), 1)
    is_re = lanes < 64
    dims = (((1,), (1,)), ((), ()))
    for q in range(out.shape[0]):
        r = pairs[q, 0]
        s = pairs[q, 1]
        total_re = jnp.zeros((BLOCK, BLOCK), jnp.float32)
        total_im = jnp.zeros((BLOCK, BLOCK), jnp.float32)
        upper = []
        rotated = []
        lower = []
        for ref in (own, sib):
            a = ref[r]
            turned = pltpu.roll(a.astype(jnp.float32), 64, 1)
            upper.append(a)
            rotated.append(jnp.where(is_re, turned, -turned).astype(a.dtype))
            lower.append(ref[s])
        a = jnp.concatenate([jnp.concatenate(upper, 1), jnp.concatenate(rotated, 1)], 0)
        b = jnp.concatenate(lower, 1)
        both = lax.dot_general(a, b, dims, preferred_element_type=jnp.float32)
        out[q, 0] = both[:BLOCK].astype(out.dtype)
        out[q, 1] = both[BLOCK:].astype(out.dtype)


def partial_sums(pairs, own, sib):
    slots = pairs.shape[0]
    return pl.pallas_call(
        products_kernel,
        out_shape=jax.ShapeDtypeStruct((slots, 2, BLOCK, BLOCK), jnp.bfloat16),
        in_specs=[
            pl.BlockSpec(memory_space=pltpu.SMEM),
            pl.BlockSpec(memory_space=pltpu.VMEM),
            pl.BlockSpec(memory_space=pltpu.VMEM),
        ],
        out_specs=pl.BlockSpec(memory_space=pltpu.VMEM),
        compiler_params=pltpu.CompilerParams(vmem_limit_bytes=32 << 20),
        name="products",
    )(pairs, own, sib)


def on_device(traces, block_pairs, valid_count):
    windows, channels, _ = traces.shape
    chips = lax.axis_size(("zh", "y"))
    cores = lax.axis_size("core")
    grouped = whitened_groups(traces)
    banded = lax.all_to_all(grouped, ("zl", "x"), split_axis=0, concat_axis=0, tiled=True)
    own = banded.reshape(-1, BLOCK, banded.shape[2])
    sib = lax.ppermute(own, "core", [(0, 1), (1, 0)])
    core = lax.axis_index("core")
    pairs = lax.dynamic_index_in_dim(block_pairs.reshape(chips, cores, 2), core, 1, keepdims=False)
    partial = partial_sums(pairs, own, sib)
    received = lax.all_to_all(partial, ("zh", "y"), split_axis=0, concat_axis=0, tiled=True)
    total = jnp.sum(received.astype(jnp.float32), axis=0)
    stack_scale = 1.0 / math.sqrt(windows * chips * cores * GROUP)
    slot = lax.axis_index(("zh", "y")) * cores + core
    live = (slot < valid_count[0]).astype(jnp.float32)
    return (total * (stack_scale * live))[None, None]


def solution(mesh):
    fine = Mesh(mesh.devices.reshape(4, 4, 2, 2, 4), ("zh", "y", "core", "zl", "x"))
    win = ("zh", "y", "core")
    chan = ("zl", "x")
    return jax.shard_map(
        on_device,
        mesh=fine,
        in_specs=(P(win, chan, None), P(), P()),
        out_specs=P(win, chan, None, None, None),
        check_vma=False,
    )
```

```python
import math

import jax
import jax.numpy as jnp
import numpy as np
from jax import lax
from jax.experimental import pallas as pl
from jax.experimental.pallas import tpu as pltpu
from jax.sharding import Mesh, PartitionSpec as P

BLOCK = 128
NBINS = 256
FREQ_LO = 64
GROUP = 32
EPS = 1e-06
QUARTERS = 4


def packed_table(length):
    times = np.arange(length // QUARTERS, dtype=np.int64)
    freqs = FREQ_LO + np.arange(NBINS, dtype=np.int64)
    angles = (times[:, None] * freqs[None, :] % length) * (2.0 * math.pi / length)
    factor = 1.0 / math.sqrt(length)
    re = (np.cos(angles) * factor).reshape(-1, NBINS // 64, 64)
    im = (-np.sin(angles) * factor).reshape(-1, NBINS // 64, 64)
    return np.concatenate([re, im], axis=2).reshape(-1, 2 * NBINS).astype(jnp.bfloat16)


def spectra_kernel(traces, table, out, table_buf, buf, sems):
    steps, windows, span, length = buf.shape
    quarter = length // QUARTERS
    load_table = pltpu.make_async_copy(table, table_buf, sems.at[steps])
    load_table.start()
    loads = []
    for step in range(steps):
        load = pltpu.make_async_copy(
            traces.at[:, pl.ds(step * span, span), :], buf.at[step], sems.at[step]
        )
        load.start()
        loads.append(load)
    lanes = lax.broadcasted_iota(jnp.int32, (span, 128), 1)
    bin4 = (FREQ_LO + lanes) % 4
    sign2 = jnp.where(bin4 % 2 == 0, 1.0, -1.0)
    direct = jnp.where(bin4 == 0, 1.0, jnp.where(bin4 == 2, -1.0, 0.0))
    up = jnp.where(bin4 == 1, 1.0, jnp.where(bin4 == 3, -1.0, 0.0))
    cross = jnp.where(lanes < 64, up, -up)
    lane32 = lanes // 32 % 2
    tiles = 2 * NBINS // 128
    load_table.wait()
    for step in range(steps):
        loads[step].wait()
        whole = buf[step].reshape(windows * span, length)
        stacked = jnp.concatenate(
            [whole[:, q * quarter : (q + 1) * quarter] for q in range(QUARTERS)], axis=0
        )
        dots = jnp.dot(stacked, table_buf[...], preferred_element_type=jnp.float32)
        spans = []
        for w in range(windows):
            parts = []
            energy = jnp.zeros((span, 1), jnp.float32)
            for t in range(tiles):
                cols = slice(t * 128, (t + 1) * 128)
                d0, d1, d2, d3 = (
                    dots[(q * windows + w) * span : (q * windows + w + 1) * span, cols]
                    for q in range(QUARTERS)
                )
                main = d0 + sign2 * d2
                turn = d1 + sign2 * d3
                full = main + direct * turn + cross * pltpu.roll(turn, 64, 1)
                energy = energy + jnp.sum(full * full, axis=1, keepdims=True)
                parts.append(full)
            scale = lax.rsqrt(energy / NBINS + EPS)
            spans.append([part * scale for part in parts])
        rows = pl.ds(step * span, span)
        for t in range(tiles):
            first, second = spans[0][t], spans[1][t]
            out[2 * t, rows] = jnp.where(lane32 == 0, first, pltpu.roll(second, 32, 1)).astype(out.dtype)
            out[2 * t + 1, rows] = jnp.where(lane32 == 1, first, pltpu.roll(second, 96, 1)).astype(
                out.dtype
            )


def in_hbm(values):
    return pltpu.with_memory_space_constraint(values, pltpu.HBM)


def whitened_groups(traces, steps=4):
    windows, channels, length = traces.shape
    table = jnp.asarray(packed_table(length))
    groups = NBINS // GROUP
    return pl.pallas_call(
        spectra_kernel,
        out_shape=jax.ShapeDtypeStruct((groups, channels, windows * 2 * GROUP), jnp.bfloat16),
        in_specs=[pl.BlockSpec(memory_space=pltpu.HBM), pl.BlockSpec(memory_space=pltpu.HBM)],
        out_specs=pl.BlockSpec(memory_space=pltpu.VMEM),
        scratch_shapes=[
            pltpu.VMEM(table.shape, table.dtype),
            pltpu.VMEM((steps, windows, channels // steps, length), traces.dtype),
            pltpu.SemaphoreType.DMA((steps + 1,)),
        ],
        compiler_params=pltpu.CompilerParams(vmem_limit_bytes=16 << 20),
        name="spectra",
    )(in_hbm(traces), in_hbm(table))


def products_kernel(pairs, own, sib, *outs):
    lanes = lax.broadcasted_iota(jnp.int32, (BLOCK, 128), 1)
    is_re = lanes < 64
    dims = (((1,), (1,)), ((), ()))
    here_z = lax.axis_index("zh")
    here_y = lax.axis_index("y")
    core = lax.axis_index("core")
    cores = lax.axis_size("core")
    for d, out in enumerate(outs):
        size_z = out.shape[0]
        for e in range(size_z):
            chip = (here_z + e) % size_z * len(outs) + (here_y + d) % len(outs)
            slot = chip * cores + core
            r = pairs[slot, 0]
            s = pairs[slot, 1]
            upper = []
            rotated = []
            lower = []
            for ref in (own, sib):
                block = ref[r]
                turned = pltpu.roll(block.astype(jnp.float32), 64, 1)
                upper.append(block)
                rotated.append(jnp.where(is_re, turned, -turned).astype(block.dtype))
                lower.append(ref[s])
            a = jnp.concatenate([jnp.concatenate(upper, 1), jnp.concatenate(rotated, 1)], 0)
            b = jnp.concatenate(lower, 1)
            both = lax.dot_general(a, b, dims, preferred_element_type=jnp.float32)
            out[e, 0] = both[:BLOCK].astype(out.dtype)
            out[e, 1] = both[BLOCK:].astype(out.dtype)


def vmem():
    return pl.BlockSpec(memory_space=pltpu.VMEM)


def partial_sums(pairs, own, sib):
    size_z = lax.axis_size("zh")
    size_y = lax.axis_size("y")
    shape = (size_z, 2, BLOCK, BLOCK)
    return pl.pallas_call(
        products_kernel,
        out_shape=[
            jax.ShapeDtypeStruct(shape, jnp.bfloat16 if d else jnp.float32) for d in range(size_y)
        ],
        in_specs=[pl.BlockSpec(memory_space=pltpu.SMEM), vmem(), vmem()],
        out_specs=[vmem()] * size_y,
        compiler_params=pltpu.CompilerParams(vmem_limit_bytes=8 << 20),
        name="products",
    )(pairs, own, sib)


def stage_kernel(*refs):
    parts = len(refs) // 2
    for e in range(parts):
        total = refs[0][e]
        for ref in refs[1:parts]:
            total = total + ref[e].astype(jnp.float32)
        refs[parts + e][...] = total.astype(refs[parts + e].dtype)


def stage_sums(arrays):
    size_z = arrays[0].shape[0]
    shape = arrays[0].shape[1:]
    return pl.pallas_call(
        stage_kernel,
        out_shape=[
            jax.ShapeDtypeStruct(shape, jnp.bfloat16 if e else jnp.float32) for e in range(size_z)
        ],
        in_specs=[vmem()] * len(arrays),
        out_specs=[vmem()] * size_z,
        compiler_params=pltpu.CompilerParams(vmem_limit_bytes=8 << 20),
        name="stage",
    )(*arrays)


def shifted(values, axis, offset):
    size = lax.axis_size(axis)
    return lax.ppermute(values, axis, [(i, (i + offset) % size) for i in range(size)])


def spread(arrays, axis):
    return [arrays[0]] + [shifted(values, axis, d) for d, values in enumerate(arrays) if d]


def on_device(traces, block_pairs, valid_count):
    windows = traces.shape[0] * lax.axis_size(("zh", "y", "core"))
    grouped = whitened_groups(traces)
    banded = lax.all_to_all(grouped, ("zl", "x"), split_axis=0, concat_axis=0, tiled=True)
    own = banded.reshape(-1, BLOCK, banded.shape[2])
    sib = shifted(own, "core", 1)
    along_y = spread(partial_sums(block_pairs, own, sib), "y")
    along_z = spread(stage_sums(along_y), "zh")
    total = along_z[0]
    for values in along_z[1:]:
        total = total + values.astype(jnp.float32)
    stack_scale = 1.0 / math.sqrt(windows * GROUP)
    slot = lax.axis_index(("zh", "y", "core"))
    live = (slot < valid_count[0]).astype(jnp.float32)
    return (total * (stack_scale * live))[None, None]


def solution(mesh):
    fine = Mesh(mesh.devices.reshape(4, 4, 2, 2, 4), ("zh", "y", "core", "zl", "x"))
    win = ("zh", "y", "core")
    chan = ("zl", "x")
    return jax.shard_map(
        on_device,
        mesh=fine,
        in_specs=(P(win, chan, None), P(), P()),
        out_specs=P(win, chan, None, None, None),
        check_vma=False,
    )
```

```python
import functools
import math

import jax
import jax.numpy as jnp
import numpy as np
from jax import lax
from jax.experimental import pallas as pl
from jax.experimental.pallas import tpu as pltpu
from jax.sharding import Mesh, PartitionSpec as P

BLOCK = 128
NBINS = 256
FREQ_LO = 64
GROUP = 32
EPS = 1e-06
QUARTERS = 4


def packed_table(length):
    times = np.arange(length // QUARTERS, dtype=np.int64)
    freqs = FREQ_LO + np.arange(NBINS, dtype=np.int64)
    angles = (times[:, None] * freqs[None, :] % length) * (2.0 * math.pi / length)
    factor = 1.0 / math.sqrt(length)
    re = (np.cos(angles) * factor).reshape(-1, NBINS // 64, 64)
    im = (-np.sin(angles) * factor).reshape(-1, NBINS // 64, 64)
    return np.concatenate([re, im], axis=2).reshape(-1, 2 * NBINS).astype(jnp.bfloat16)


def spectra_kernel(traces, table, out, table_buf, buf, sems):
    steps, windows, span, length = buf.shape
    quarter = length // QUARTERS
    load_table = pltpu.make_async_copy(table, table_buf, sems.at[steps])
    load_table.start()
    loads = []
    for step in range(steps):
        load = pltpu.make_async_copy(
            traces.at[:, pl.ds(step * span, span), :], buf.at[step], sems.at[step]
        )
        load.start()
        loads.append(load)
    lanes = lax.broadcasted_iota(jnp.int32, (span, 128), 1)
    bin4 = (FREQ_LO + lanes) % 4
    sign2 = jnp.where(bin4 % 2 == 0, 1.0, -1.0)
    direct = jnp.where(bin4 == 0, 1.0, jnp.where(bin4 == 2, -1.0, 0.0))
    up = jnp.where(bin4 == 1, 1.0, jnp.where(bin4 == 3, -1.0, 0.0))
    cross = jnp.where(lanes < 64, up, -up)
    lane32 = lanes // 32 % 2
    tiles = 2 * NBINS // 128
    load_table.wait()
    for step in range(steps):
        loads[step].wait()
        whole = buf[step].reshape(windows * span, length)
        stacked = jnp.concatenate(
            [whole[:, q * quarter : (q + 1) * quarter] for q in range(QUARTERS)], axis=0
        )
        dots = jnp.dot(stacked, table_buf[...], preferred_element_type=jnp.float32)
        spans = []
        for w in range(windows):
            parts = []
            energy = jnp.zeros((span, 1), jnp.float32)
            for t in range(tiles):
                cols = slice(t * 128, (t + 1) * 128)
                d0, d1, d2, d3 = (
                    dots[(q * windows + w) * span : (q * windows + w + 1) * span, cols]
                    for q in range(QUARTERS)
                )
                main = d0 + sign2 * d2
                turn = d1 + sign2 * d3
                full = main + direct * turn + cross * pltpu.roll(turn, 64, 1)
                energy = energy + jnp.sum(full * full, axis=1, keepdims=True)
                parts.append(full)
            scale = lax.rsqrt(energy / NBINS + EPS)
            spans.append([part * scale for part in parts])
        rows = pl.ds(step * span, span)
        for t in range(tiles):
            first, second = spans[0][t], spans[1][t]
            out[2 * t, rows] = jnp.where(lane32 == 0, first, pltpu.roll(second, 32, 1)).astype(out.dtype)
            out[2 * t + 1, rows] = jnp.where(lane32 == 1, first, pltpu.roll(second, 96, 1)).astype(
                out.dtype
            )


def in_hbm(values):
    return pltpu.with_memory_space_constraint(values, pltpu.HBM)


def whitened_groups(traces, steps=4):
    windows, channels, length = traces.shape
    table = jnp.asarray(packed_table(length))
    groups = NBINS // GROUP
    return pl.pallas_call(
        spectra_kernel,
        out_shape=jax.ShapeDtypeStruct((groups, channels, windows * 2 * GROUP), jnp.bfloat16),
        in_specs=[pl.BlockSpec(memory_space=pltpu.HBM), pl.BlockSpec(memory_space=pltpu.HBM)],
        out_specs=pl.BlockSpec(memory_space=pltpu.VMEM),
        scratch_shapes=[
            pltpu.VMEM(table.shape, table.dtype),
            pltpu.VMEM((steps, windows, channels // steps, length), traces.dtype),
            pltpu.SemaphoreType.DMA((steps + 1,)),
        ],
        compiler_params=pltpu.CompilerParams(vmem_limit_bytes=16 << 20),
        name="spectra",
    )(in_hbm(traces), in_hbm(table))


def products_kernel(offset, pairs, own, sib, out):
    lanes = lax.broadcasted_iota(jnp.int32, (BLOCK, 128), 1)
    is_re = lanes < 64
    dims = (((1,), (1,)), ((), ()))
    size_z = lax.axis_size("zh")
    size_y = lax.axis_size("y")
    cores = lax.axis_size("core")
    to_y = (lax.axis_index("y") + offset) % size_y
    for e in range(size_z):
        to_z = (lax.axis_index("zh") + e) % size_z
        slot = (to_z * size_y + to_y) * cores + lax.axis_index("core")
        r = pairs[slot, 0]
        s = pairs[slot, 1]
        upper = []
        rotated = []
        lower = []
        for ref in (own, sib):
            block = ref[r]
            turned = pltpu.roll(block.astype(jnp.float32), 64, 1)
            upper.append(block)
            rotated.append(jnp.where(is_re, turned, -turned).astype(block.dtype))
            lower.append(ref[s])
        a = jnp.concatenate([jnp.concatenate(upper, 1), jnp.concatenate(rotated, 1)], 0)
        b = jnp.concatenate(lower, 1)
        both = lax.dot_general(a, b, dims, preferred_element_type=jnp.float32)
        out[e, 0] = both[:BLOCK].astype(out.dtype)
        out[e, 1] = both[BLOCK:].astype(out.dtype)


def vmem():
    return pl.BlockSpec(memory_space=pltpu.VMEM)


def partial_sums(offset, pairs, own, sib):
    shape = (lax.axis_size("zh"), 2, BLOCK, BLOCK)
    return pl.pallas_call(
        functools.partial(products_kernel, offset),
        out_shape=jax.ShapeDtypeStruct(shape, jnp.bfloat16 if offset else jnp.float32),
        in_specs=[pl.BlockSpec(memory_space=pltpu.SMEM), vmem(), vmem()],
        out_specs=vmem(),
        compiler_params=pltpu.CompilerParams(vmem_limit_bytes=8 << 20),
        name="products",
    )(pairs, own, sib)


def stage_kernel(*refs):
    parts = len(refs) // 2
    for e in range(parts):
        total = refs[0][e]
        for ref in refs[1:parts]:
            total = total + ref[e].astype(jnp.float32)
        refs[parts + e][...] = total.astype(refs[parts + e].dtype)


def stage_sums(arrays):
    size_z = arrays[0].shape[0]
    shape = arrays[0].shape[1:]
    return pl.pallas_call(
        stage_kernel,
        out_shape=[
            jax.ShapeDtypeStruct(shape, jnp.bfloat16 if e else jnp.float32) for e in range(size_z)
        ],
        in_specs=[vmem()] * len(arrays),
        out_specs=[vmem()] * size_z,
        compiler_params=pltpu.CompilerParams(vmem_limit_bytes=8 << 20),
        name="stage",
    )(*arrays)


def shifted(values, axis, offset):
    size = lax.axis_size(axis)
    return lax.ppermute(values, axis, [(i, (i + offset) % size) for i in range(size)])


def far_first(size):
    return sorted(range(1, size), key=lambda d: -min(d, size - d))


def on_device(traces, block_pairs, valid_count):
    windows = traces.shape[0] * lax.axis_size(("zh", "y", "core"))
    grouped = whitened_groups(traces)
    banded = lax.all_to_all(grouped, ("zl", "x"), split_axis=0, concat_axis=0, tiled=True)
    own = banded.reshape(-1, BLOCK, banded.shape[2])
    sib = shifted(own, "core", 1)
    arrived = []
    for d in far_first(lax.axis_size("y")):
        arrived.append(shifted(partial_sums(d, block_pairs, own, sib), "y", d))
    staged = stage_sums([partial_sums(0, block_pairs, own, sib)] + arrived)
    total = staged[0]
    for values in [shifted(staged[e], "zh", e) for e in far_first(len(staged))]:
        total = total + values.astype(jnp.float32)
    stack_scale = 1.0 / math.sqrt(windows * GROUP)
    slot = lax.axis_index(("zh", "y", "core"))
    live = (slot < valid_count[0]).astype(jnp.float32)
    return (total * (stack_scale * live))[None, None]


def solution(mesh):
    fine = Mesh(mesh.devices.reshape(4, 4, 2, 2, 4), ("zh", "y", "core", "zl", "x"))
    win = ("zh", "y", "core")
    chan = ("zl", "x")
    return jax.shard_map(
        on_device,
        mesh=fine,
        in_specs=(P(win, chan, None), P(), P()),
        out_specs=P(win, chan, None, None, None),
        check_vma=False,
    )
```

```python
import math

import jax
import jax.numpy as jnp
import numpy as np
from jax import lax
from jax.experimental import pallas as pl
from jax.experimental.pallas import tpu as pltpu
from jax.sharding import Mesh, PartitionSpec as P

BLOCK = 128
NBINS = 256
FREQ_LO = 64
GROUP = 32
EPS = 1e-06
QUARTERS = 4
ROWS = 32


def packed_table(length):
    times = np.arange(length // QUARTERS, dtype=np.int64)
    freqs = FREQ_LO + np.arange(NBINS, dtype=np.int64)
    angles = (times[:, None] * freqs[None, :] % length) * (2.0 * math.pi / length)
    factor = 1.0 / math.sqrt(length)
    re = (np.cos(angles) * factor).reshape(-1, NBINS // 64, 64)
    im = (-np.sin(angles) * factor).reshape(-1, NBINS // 64, 64)
    return np.concatenate([re, im], axis=2).reshape(-1, 2 * NBINS).astype(jnp.bfloat16)


def spectra_kernel(traces, table, out, table_buf, buf, sems):
    steps, windows, span, length = buf.shape
    quarter = length // QUARTERS
    load_table = pltpu.make_async_copy(table, table_buf, sems.at[steps])
    load_table.start()
    loads = []
    for step in range(steps):
        load = pltpu.make_async_copy(
            traces.at[:, pl.ds(step * span, span), :], buf.at[step], sems.at[step]
        )
        load.start()
        loads.append(load)
    lanes = lax.broadcasted_iota(jnp.int32, (1, 128), 1)
    bin4 = (FREQ_LO + lanes) % 4
    sign2 = jnp.where(bin4 % 2 == 0, 1.0, -1.0)
    direct = jnp.where(bin4 == 0, 1.0, jnp.where(bin4 == 2, -1.0, 0.0))
    up = jnp.where(bin4 == 1, 1.0, jnp.where(bin4 == 3, -1.0, 0.0))
    cross = jnp.where(lanes < 64, up, -up)
    lane32 = lanes // 32 % 2
    tiles = 2 * NBINS // 128

    def finish(step, dots):
        for start in range(0, span, ROWS):
            spans = []
            for w in range(windows):
                parts = []
                squares = jnp.zeros((ROWS, 128), jnp.float32)
                for t in range(tiles):
                    first_rows = [(q * windows + w) * span + start for q in range(QUARTERS)]
                    d0, d1, d2, d3 = (
                        dots[row : row + ROWS, t * 128 : (t + 1) * 128] for row in first_rows
                    )
                    main = d0 + sign2 * d2
                    turn = d1 + sign2 * d3
                    full = main + direct * turn + cross * pltpu.roll(turn, 64, 1)
                    squares = squares + full * full
                    parts.append(full)
                energy = jnp.sum(squares, axis=1, keepdims=True)
                scale = lax.rsqrt(energy / NBINS + EPS)
                spans.append([part * scale for part in parts])
            rows = pl.ds(step * span + start, ROWS)
            for t in range(tiles):
                first, second = spans[0][t], spans[1][t]
                even = jnp.where(lane32 == 0, first, pltpu.roll(second, 32, 1))
                odd = jnp.where(lane32 == 1, first, pltpu.roll(second, 96, 1))
                out[2 * t, rows] = even.astype(out.dtype)
                out[2 * t + 1, rows] = odd.astype(out.dtype)

    load_table.wait()
    before = None
    for step in range(steps):
        loads[step].wait()
        whole = buf[step].reshape(windows * span, length)
        stacked = jnp.concatenate(
            [whole[:, q * quarter : (q + 1) * quarter] for q in range(QUARTERS)], axis=0
        )
        dots = jnp.dot(stacked, table_buf[...], preferred_element_type=jnp.float32)
        if step:
            finish(step - 1, before)
        before = dots
    finish(steps - 1, before)


def in_hbm(values):
    return pltpu.with_memory_space_constraint(values, pltpu.HBM)


def whitened_groups(traces, steps=4):
    windows, channels, length = traces.shape
    table = jnp.asarray(packed_table(length))
    groups = NBINS // GROUP
    return pl.pallas_call(
        spectra_kernel,
        out_shape=jax.ShapeDtypeStruct((groups, channels, windows * 2 * GROUP), jnp.bfloat16),
        in_specs=[pl.BlockSpec(memory_space=pltpu.HBM), pl.BlockSpec(memory_space=pltpu.HBM)],
        out_specs=pl.BlockSpec(memory_space=pltpu.VMEM),
        scratch_shapes=[
            pltpu.VMEM(table.shape, table.dtype),
            pltpu.VMEM((steps, windows, channels // steps, length), traces.dtype),
            pltpu.SemaphoreType.DMA((steps + 1,)),
        ],
        compiler_params=pltpu.CompilerParams(vmem_limit_bytes=16 << 20),
        name="spectra",
    )(in_hbm(traces), in_hbm(table))


def products_kernel(pairs, own, sib, *outs):
    lanes = lax.broadcasted_iota(jnp.int32, (BLOCK, 128), 1)
    is_re = lanes < 64
    dims = (((1,), (1,)), ((), ()))
    here_z = lax.axis_index("zh")
    here_y = lax.axis_index("y")
    core = lax.axis_index("core")
    cores = lax.axis_size("core")
    for d, out in enumerate(outs):
        size_z = out.shape[0]
        for e in range(size_z):
            chip = (here_z + e) % size_z * len(outs) + (here_y + d) % len(outs)
            slot = chip * cores + core
            r = pairs[slot, 0]
            s = pairs[slot, 1]
            upper = []
            rotated = []
            lower = []
            for ref in (own, sib):
                block = ref[r]
                turned = pltpu.roll(block.astype(jnp.float32), 64, 1)
                upper.append(block)
                rotated.append(jnp.where(is_re, turned, -turned).astype(block.dtype))
                lower.append(ref[s])
            a = jnp.concatenate([jnp.concatenate(upper, 1), jnp.concatenate(rotated, 1)], 0)
            b = jnp.concatenate(lower, 1)
            both = lax.dot_general(a, b, dims, preferred_element_type=jnp.float32)
            out[e, 0] = both[:BLOCK].astype(out.dtype)
            out[e, 1] = both[BLOCK:].astype(out.dtype)


def vmem():
    return pl.BlockSpec(memory_space=pltpu.VMEM)


def partial_sums(pairs, own, sib):
    size_z = lax.axis_size("zh")
    size_y = lax.axis_size("y")
    shape = (size_z, 2, BLOCK, BLOCK)
    return pl.pallas_call(
        products_kernel,
        out_shape=[
            jax.ShapeDtypeStruct(shape, jnp.bfloat16 if d else jnp.float32) for d in range(size_y)
        ],
        in_specs=[pl.BlockSpec(memory_space=pltpu.SMEM), vmem(), vmem()],
        out_specs=[vmem()] * size_y,
        compiler_params=pltpu.CompilerParams(vmem_limit_bytes=8 << 20),
        name="products",
    )(pairs, own, sib)


def stage_kernel(*refs):
    parts = len(refs) // 2
    for e in range(parts):
        total = refs[0][e]
        for ref in refs[1:parts]:
            total = total + ref[e].astype(jnp.float32)
        refs[parts + e][...] = total.astype(refs[parts + e].dtype)


def stage_sums(arrays):
    size_z = arrays[0].shape[0]
    shape = arrays[0].shape[1:]
    return pl.pallas_call(
        stage_kernel,
        out_shape=[
            jax.ShapeDtypeStruct(shape, jnp.bfloat16 if e else jnp.float32) for e in range(size_z)
        ],
        in_specs=[vmem()] * len(arrays),
        out_specs=[vmem()] * size_z,
        compiler_params=pltpu.CompilerParams(vmem_limit_bytes=8 << 20),
        name="stage",
    )(*arrays)


def shifted(values, axis, offset):
    size = lax.axis_size(axis)
    return lax.ppermute(values, axis, [(i, (i + offset) % size) for i in range(size)])


def spread(arrays, axis):
    size = len(arrays)
    order = sorted(range(1, size), key=lambda d: -min(d, size - d))
    return [arrays[0]] + [shifted(arrays[d], axis, d) for d in order]


def on_device(traces, block_pairs, valid_count):
    windows = traces.shape[0] * lax.axis_size(("zh", "y", "core"))
    grouped = whitened_groups(traces)
    banded = lax.all_to_all(grouped, ("zl", "x"), split_axis=0, concat_axis=0, tiled=True)
    own = banded.reshape(-1, BLOCK, banded.shape[2])
    sib = shifted(own, "core", 1)
    along_y = spread(partial_sums(block_pairs, own, sib), "y")
    along_z = spread(stage_sums(along_y), "zh")
    total = along_z[0]
    for values in along_z[1:]:
        total = total + values.astype(jnp.float32)
    stack_scale = 1.0 / math.sqrt(windows * GROUP)
    slot = lax.axis_index(("zh", "y", "core"))
    live = (slot < valid_count[0]).astype(jnp.float32)
    return (total * (stack_scale * live))[None, None]


def solution(mesh):
    fine = Mesh(mesh.devices.reshape(4, 4, 2, 2, 4), ("zh", "y", "core", "zl", "x"))
    win = ("zh", "y", "core")
    chan = ("zl", "x")
    return jax.shard_map(
        on_device,
        mesh=fine,
        in_specs=(P(win, chan, None), P(), P()),
        out_specs=P(win, chan, None, None, None),
        check_vma=False,
    )
```

```python
import math

import jax
import jax.numpy as jnp
import numpy as np
from jax import lax
from jax.experimental import pallas as pl
from jax.experimental.pallas import tpu as pltpu
from jax.sharding import Mesh, PartitionSpec as P

BLOCK = 128
NBINS = 256
FREQ_LO = 64
GROUP = 32
EPS = 1e-06
QUARTERS = 4
ROWS = 32


def packed_table(length):
    times = np.arange(length // QUARTERS, dtype=np.int64)
    freqs = FREQ_LO + np.arange(NBINS, dtype=np.int64)
    angles = (times[:, None] * freqs[None, :] % length) * (2.0 * math.pi / length)
    factor = 1.0 / math.sqrt(length)
    re = (np.cos(angles) * factor).reshape(-1, NBINS // 64, 64)
    im = (-np.sin(angles) * factor).reshape(-1, NBINS // 64, 64)
    return np.concatenate([re, im], axis=2).reshape(-1, 2 * NBINS).astype(jnp.bfloat16)


def spectra_kernel(traces, table, out, table_buf, buf, sems):
    steps, windows, span, length = buf.shape
    quarter = length // QUARTERS
    load_table = pltpu.make_async_copy(table, table_buf, sems.at[steps])
    load_table.start()
    loads = []
    for step in range(steps):
        load = pltpu.make_async_copy(
            traces.at[:, pl.ds(step * span, span), :], buf.at[step], sems.at[step]
        )
        load.start()
        loads.append(load)
    lanes = lax.broadcasted_iota(jnp.int32, (1, 128), 1)
    bin4 = (FREQ_LO + lanes) % 4
    sign2 = jnp.where(bin4 % 2 == 0, 1.0, -1.0)
    direct = jnp.where(bin4 == 0, 1.0, jnp.where(bin4 == 2, -1.0, 0.0))
    up = jnp.where(bin4 == 1, 1.0, jnp.where(bin4 == 3, -1.0, 0.0))
    cross = jnp.where(lanes < 64, up, -up)
    lane32 = lanes // 32 % 2
    tiles = 2 * NBINS // 128

    def finish(step, dots):
        for start in range(0, span, ROWS):
            spans = []
            for w in range(windows):
                parts = []
                squares = jnp.zeros((ROWS, 128), jnp.float32)
                for t in range(tiles):
                    first_rows = [(q * windows + w) * span + start for q in range(QUARTERS)]
                    d0, d1, d2, d3 = (
                        dots[row : row + ROWS, t * 128 : (t + 1) * 128] for row in first_rows
                    )
                    main = d0 + sign2 * d2
                    turn = d1 + sign2 * d3
                    full = main + direct * turn + cross * pltpu.roll(turn, 64, 1)
                    squares = squares + full * full
                    parts.append(full)
                energy = jnp.sum(squares, axis=1, keepdims=True)
                scale = lax.rsqrt(energy / NBINS + EPS)
                spans.append([part * scale for part in parts])
            rows = pl.ds(step * span + start, ROWS)
            for t in range(tiles):
                first, second = spans[0][t], spans[1][t]
                even = jnp.where(lane32 == 0, first, pltpu.roll(second, 32, 1))
                odd = jnp.where(lane32 == 1, first, pltpu.roll(second, 96, 1))
                out[2 * t, rows] = even.astype(out.dtype)
                out[2 * t + 1, rows] = odd.astype(out.dtype)

    load_table.wait()
    before = None
    for step in range(steps):
        loads[step].wait()
        whole = buf[step].reshape(windows * span, length)
        stacked = jnp.concatenate(
            [whole[:, q * quarter : (q + 1) * quarter] for q in range(QUARTERS)], axis=0
        )
        dots = jnp.dot(stacked, table_buf[...], preferred_element_type=jnp.float32)
        if step:
            finish(step - 1, before)
        before = dots
    finish(steps - 1, before)


def in_hbm(values):
    return pltpu.with_memory_space_constraint(values, pltpu.HBM)


def whitened_groups(traces, steps=4):
    windows, channels, length = traces.shape
    table = jnp.asarray(packed_table(length))
    groups = NBINS // GROUP
    return pl.pallas_call(
        spectra_kernel,
        out_shape=jax.ShapeDtypeStruct((groups, channels, windows * 2 * GROUP), jnp.bfloat16),
        in_specs=[pl.BlockSpec(memory_space=pltpu.HBM), pl.BlockSpec(memory_space=pltpu.HBM)],
        out_specs=pl.BlockSpec(memory_space=pltpu.VMEM),
        scratch_shapes=[
            pltpu.VMEM(table.shape, table.dtype),
            pltpu.VMEM((steps, windows, channels // steps, length), traces.dtype),
            pltpu.SemaphoreType.DMA((steps + 1,)),
        ],
        compiler_params=pltpu.CompilerParams(vmem_limit_bytes=16 << 20),
        name="spectra",
    )(in_hbm(traces), in_hbm(table))


def products_kernel(pairs, own, sib, *outs):
    lanes = lax.broadcasted_iota(jnp.int32, (BLOCK, 128), 1)
    is_re = lanes < 64
    dims = (((1,), (1,)), ((), ()))
    here_z = lax.axis_index("zh")
    here_y = lax.axis_index("y")
    core = lax.axis_index("core")
    cores = lax.axis_size("core")
    size_z = lax.axis_size("zh")
    size_y = lax.axis_size("y")
    for e in range(size_z):
        for d in range(size_y):
            chip = (here_z + e) % size_z * size_y + (here_y + d) % size_y
            slot = chip * cores + core
            r = pairs[slot, 0]
            s = pairs[slot, 1]
            upper = []
            rotated = []
            lower = []
            for ref in (own, sib):
                block = ref[r]
                turned = pltpu.roll(block.astype(jnp.float32), 64, 1)
                upper.append(block)
                rotated.append(jnp.where(is_re, turned, -turned).astype(block.dtype))
                lower.append(ref[s])
            a = jnp.concatenate([jnp.concatenate(upper, 1), jnp.concatenate(rotated, 1)], 0)
            b = jnp.concatenate(lower, 1)
            both = lax.dot_general(a, b, dims, preferred_element_type=jnp.float32)
            out = outs[size_y + d].at[e - 1] if e else outs[d]
            out[0] = both[:BLOCK].astype(out.dtype)
            out[1] = both[BLOCK:].astype(out.dtype)


def vmem():
    return pl.BlockSpec(memory_space=pltpu.VMEM)


def partial_sums(pairs, own, sib):
    size_z = lax.axis_size("zh")
    size_y = lax.axis_size("y")
    shape = (2, BLOCK, BLOCK)
    types = [jnp.bfloat16 if d else jnp.float32 for d in range(size_y)]
    outs = pl.pallas_call(
        products_kernel,
        out_shape=[jax.ShapeDtypeStruct(shape, dtype) for dtype in types]
        + [jax.ShapeDtypeStruct((size_z - 1,) + shape, dtype) for dtype in types],
        in_specs=[pl.BlockSpec(memory_space=pltpu.SMEM), vmem(), vmem()],
        out_specs=[vmem()] * (2 * size_y),
        compiler_params=pltpu.CompilerParams(vmem_limit_bytes=8 << 20),
        name="products",
    )(pairs, own, sib)
    return outs[:size_y], outs[size_y:]


def stage_kernel(*refs):
    came = refs[0].shape[0]
    for e in range(came):
        total = refs[0][e]
        for ref in refs[1:-came]:
            total = total + ref[e].astype(jnp.float32)
        out = refs[e - came]
        out[...] = total.astype(out.dtype)


def stage_sums(arrays):
    parts = arrays[0].shape[0]
    shape = arrays[0].shape[1:]
    return pl.pallas_call(
        stage_kernel,
        out_shape=[jax.ShapeDtypeStruct(shape, jnp.bfloat16)] * parts,
        in_specs=[vmem()] * len(arrays),
        out_specs=[vmem()] * parts,
        compiler_params=pltpu.CompilerParams(vmem_limit_bytes=8 << 20),
        name="stage",
    )(*arrays)


def shifted(values, axis, offset):
    size = lax.axis_size(axis)
    return lax.ppermute(values, axis, [(i, (i + offset) % size) for i in range(size)])


def spread(arrays, axis):
    size = len(arrays)
    order = sorted(range(1, size), key=lambda d: -min(d, size - d))
    return [arrays[0]] + [shifted(arrays[d], axis, d) for d in order]


def on_device(traces, block_pairs, valid_count):
    windows = traces.shape[0] * lax.axis_size(("zh", "y", "core"))
    grouped = whitened_groups(traces)
    banded = lax.all_to_all(grouped, ("zl", "x"), split_axis=0, concat_axis=0, tiled=True)
    own = banded.reshape(-1, BLOCK, banded.shape[2])
    sib = shifted(own, "core", 1)
    staying, going = partial_sums(block_pairs, own, sib)
    going = spread(going, "y")
    staying = spread(staying, "y")
    along_z = spread([None, *stage_sums(going)], "zh")
    total = staying[0]
    for values in staying[1:] + along_z[1:]:
        total = total + values.astype(jnp.float32)
    stack_scale = 1.0 / math.sqrt(windows * GROUP)
    slot = lax.axis_index(("zh", "y", "core"))
    live = (slot < valid_count[0]).astype(jnp.float32)
    return (total * (stack_scale * live))[None, None]


def solution(mesh):
    fine = Mesh(mesh.devices.reshape(4, 4, 2, 2, 4), ("zh", "y", "core", "zl", "x"))
    win = ("zh", "y", "core")
    chan = ("zl", "x")
    return jax.shard_map(
        on_device,
        mesh=fine,
        in_specs=(P(win, chan, None), P(), P()),
        out_specs=P(win, chan, None, None, None),
        check_vma=False,
    )
```

```python
import functools
import math

import jax
import jax.numpy as jnp
import numpy as np
from jax import lax
from jax.experimental import pallas as pl
from jax.experimental.pallas import tpu as pltpu
from jax.sharding import Mesh, PartitionSpec as P

BLOCK = 128
NBINS = 256
FREQ_LO = 64
GROUP = 32
EPS = 1e-06
QUARTERS = 4
ROWS = 32
Z_GROUPS = ((2, 1), (3, 0))


def packed_table(length):
    times = np.arange(length // QUARTERS, dtype=np.int64)
    freqs = FREQ_LO + np.arange(NBINS, dtype=np.int64)
    angles = (times[:, None] * freqs[None, :] % length) * (2.0 * math.pi / length)
    factor = 1.0 / math.sqrt(length)
    re = (np.cos(angles) * factor).reshape(-1, NBINS // 64, 64)
    im = (-np.sin(angles) * factor).reshape(-1, NBINS // 64, 64)
    return np.concatenate([re, im], axis=2).reshape(-1, 2 * NBINS).astype(jnp.bfloat16)


def spectra_kernel(traces, table, out, table_buf, buf, sems):
    steps, windows, span, length = buf.shape
    quarter = length // QUARTERS
    load_table = pltpu.make_async_copy(table, table_buf, sems.at[steps])
    load_table.start()
    loads = []
    for step in range(steps):
        load = pltpu.make_async_copy(
            traces.at[:, pl.ds(step * span, span), :], buf.at[step], sems.at[step]
        )
        load.start()
        loads.append(load)
    lanes = lax.broadcasted_iota(jnp.int32, (1, 128), 1)
    bin4 = (FREQ_LO + lanes) % 4
    sign2 = jnp.where(bin4 % 2 == 0, 1.0, -1.0)
    direct = jnp.where(bin4 == 0, 1.0, jnp.where(bin4 == 2, -1.0, 0.0))
    up = jnp.where(bin4 == 1, 1.0, jnp.where(bin4 == 3, -1.0, 0.0))
    cross = jnp.where(lanes < 64, up, -up)
    lane32 = lanes // 32 % 2
    tiles = 2 * NBINS // 128

    def finish(step, dots):
        for start in range(0, span, ROWS):
            spans = []
            for w in range(windows):
                parts = []
                squares = jnp.zeros((ROWS, 128), jnp.float32)
                for t in range(tiles):
                    first_rows = [(q * windows + w) * span + start for q in range(QUARTERS)]
                    d0, d1, d2, d3 = (
                        dots[row : row + ROWS, t * 128 : (t + 1) * 128] for row in first_rows
                    )
                    main = d0 + sign2 * d2
                    turn = d1 + sign2 * d3
                    full = main + direct * turn + cross * pltpu.roll(turn, 64, 1)
                    squares = squares + full * full
                    parts.append(full)
                energy = jnp.sum(squares, axis=1, keepdims=True)
                scale = lax.rsqrt(energy / NBINS + EPS)
                spans.append([part * scale for part in parts])
            rows = pl.ds(step * span + start, ROWS)
            for t in range(tiles):
                first, second = spans[0][t], spans[1][t]
                even = jnp.where(lane32 == 0, first, pltpu.roll(second, 32, 1))
                odd = jnp.where(lane32 == 1, first, pltpu.roll(second, 96, 1))
                out[2 * t, rows] = even.astype(out.dtype)
                out[2 * t + 1, rows] = odd.astype(out.dtype)

    load_table.wait()
    before = None
    for step in range(steps):
        loads[step].wait()
        whole = buf[step].reshape(windows * span, length)
        stacked = jnp.concatenate(
            [whole[:, q * quarter : (q + 1) * quarter] for q in range(QUARTERS)], axis=0
        )
        dots = jnp.dot(stacked, table_buf[...], preferred_element_type=jnp.float32)
        if step:
            finish(step - 1, before)
        before = dots
    finish(steps - 1, before)


def in_hbm(values):
    return pltpu.with_memory_space_constraint(values, pltpu.HBM)


def whitened_groups(traces, steps=4):
    windows, channels, length = traces.shape
    table = jnp.asarray(packed_table(length))
    groups = NBINS // GROUP
    return pl.pallas_call(
        spectra_kernel,
        out_shape=jax.ShapeDtypeStruct((groups, channels, windows * 2 * GROUP), jnp.bfloat16),
        in_specs=[pl.BlockSpec(memory_space=pltpu.HBM), pl.BlockSpec(memory_space=pltpu.HBM)],
        out_specs=pl.BlockSpec(memory_space=pltpu.VMEM),
        scratch_shapes=[
            pltpu.VMEM(table.shape, table.dtype),
            pltpu.VMEM((steps, windows, channels // steps, length), traces.dtype),
            pltpu.SemaphoreType.DMA((steps + 1,)),
        ],
        compiler_params=pltpu.CompilerParams(vmem_limit_bytes=16 << 20),
        name="spectra",
    )(in_hbm(traces), in_hbm(table))


def products_kernel(groups, pairs, own, sib, *outs):
    lanes = lax.broadcasted_iota(jnp.int32, (BLOCK, 128), 1)
    is_re = lanes < 64
    dims = (((1,), (1,)), ((), ()))
    here_z = lax.axis_index("zh")
    here_y = lax.axis_index("y")
    core = lax.axis_index("core")
    cores = lax.axis_size("core")
    size_z = lax.axis_size("zh")
    size_y = lax.axis_size("y")
    for n, out in enumerate(outs):
        for i, e in enumerate(groups[n // size_y]):
            chip = (here_z + e) % size_z * size_y + (here_y + n % size_y) % size_y
            slot = chip * cores + core
            r = pairs[slot, 0]
            s = pairs[slot, 1]
            upper = []
            rotated = []
            lower = []
            for ref in (own, sib):
                block = ref[r]
                turned = pltpu.roll(block.astype(jnp.float32), 64, 1)
                upper.append(block)
                rotated.append(jnp.where(is_re, turned, -turned).astype(block.dtype))
                lower.append(ref[s])
            a = jnp.concatenate([jnp.concatenate(upper, 1), jnp.concatenate(rotated, 1)], 0)
            b = jnp.concatenate(lower, 1)
            both = lax.dot_general(a, b, dims, preferred_element_type=jnp.float32)
            out[i, 0] = both[:BLOCK].astype(out.dtype)
            out[i, 1] = both[BLOCK:].astype(out.dtype)


def vmem():
    return pl.BlockSpec(memory_space=pltpu.VMEM)


def partial_sums(groups, pairs, own, sib):
    size_y = lax.axis_size("y")
    outs = pl.pallas_call(
        functools.partial(products_kernel, groups),
        out_shape=[
            jax.ShapeDtypeStruct(
                (len(group), 2, BLOCK, BLOCK), jnp.bfloat16 if d else jnp.float32
            )
            for group in groups
            for d in range(size_y)
        ],
        in_specs=[pl.BlockSpec(memory_space=pltpu.SMEM), vmem(), vmem()],
        out_specs=[vmem()] * (len(groups) * size_y),
        compiler_params=pltpu.CompilerParams(vmem_limit_bytes=8 << 20),
        name="products",
    )(pairs, own, sib)
    return [outs[g * size_y : (g + 1) * size_y] for g in range(len(groups))]


def stage_kernel(*refs):
    came = refs[0].shape[0]
    for i in range(came):
        total = refs[0][i]
        for ref in refs[1:-came]:
            total = total + ref[i].astype(jnp.float32)
        out = refs[i - came]
        out[...] = total.astype(out.dtype)


def stage_sums(group, arrays):
    parts = len(group)
    shape = arrays[0].shape[1:]
    return pl.pallas_call(
        stage_kernel,
        out_shape=[jax.ShapeDtypeStruct(shape, jnp.bfloat16 if e else jnp.float32) for e in group],
        in_specs=[vmem()] * len(arrays),
        out_specs=[vmem()] * parts,
        compiler_params=pltpu.CompilerParams(vmem_limit_bytes=8 << 20),
        name="stage",
    )(*arrays)


def shifted(values, axis, offset):
    size = lax.axis_size(axis)
    return lax.ppermute(values, axis, [(i, (i + offset) % size) for i in range(size)])


def far_first(size):
    ways = [min(d, size - d) for d in range(size)]
    return [[d for d in range(size) if ways[d] == way] for way in sorted(set(ways), reverse=True)]


def spread(arrays, axis):
    order = [d for group in far_first(len(arrays)) for d in group if d]
    return [arrays[0]] + [shifted(arrays[d], axis, d) for d in order]


def on_device(traces, block_pairs, valid_count):
    windows = traces.shape[0] * lax.axis_size(("zh", "y", "core"))
    grouped = whitened_groups(traces)
    banded = lax.all_to_all(grouped, ("zl", "x"), split_axis=0, concat_axis=0, tiled=True)
    own = banded.reshape(-1, BLOCK, banded.shape[2])
    sib = shifted(own, "core", 1)
    parts = []
    for group, arrays in zip(Z_GROUPS, partial_sums(Z_GROUPS, block_pairs, own, sib)):
        along_y = spread(arrays, "y")
        staged = stage_sums(group, along_y)
        parts += [shifted(values, "zh", e) if e else values for e, values in zip(group, staged)]
    total = parts[0].astype(jnp.float32)
    for values in parts[1:]:
        total = total + values.astype(jnp.float32)
    stack_scale = 1.0 / math.sqrt(windows * GROUP)
    slot = lax.axis_index(("zh", "y", "core"))
    live = (slot < valid_count[0]).astype(jnp.float32)
    return (total * (stack_scale * live))[None, None]


def solution(mesh):
    fine = Mesh(mesh.devices.reshape(4, 4, 2, 2, 4), ("zh", "y", "core", "zl", "x"))
    win = ("zh", "y", "core")
    chan = ("zl", "x")
    return jax.shard_map(
        on_device,
        mesh=fine,
        in_specs=(P(win, chan, None), P(), P()),
        out_specs=P(win, chan, None, None, None),
        check_vma=False,
    )
```

```python
import functools
import math

import jax
import jax.numpy as jnp
import numpy as np
from jax import lax
from jax.experimental import pallas as pl
from jax.experimental.pallas import tpu as pltpu
from jax.sharding import Mesh, PartitionSpec as P

BLOCK = 128
NBINS = 256
FREQ_LO = 64
GROUP = 32
EPS = 1e-06
QUARTERS = 4
ROWS = 32
Z_GROUPS = ((2, 1), (3, 0))


def packed_table(length):
    times = np.arange(length // QUARTERS, dtype=np.int64)
    freqs = FREQ_LO + np.arange(NBINS, dtype=np.int64)
    angles = (times[:, None] * freqs[None, :] % length) * (2.0 * math.pi / length)
    factor = 1.0 / math.sqrt(length)
    re = (np.cos(angles) * factor).reshape(-1, NBINS // 64, 64)
    im = (-np.sin(angles) * factor).reshape(-1, NBINS // 64, 64)
    return np.concatenate([re, im], axis=2).reshape(-1, 2 * NBINS).astype(jnp.bfloat16)


def spectra_kernel(traces, table, out, table_buf, buf, sems):
    steps, windows, span, length = buf.shape
    quarter = length // QUARTERS
    load_table = pltpu.make_async_copy(table, table_buf, sems.at[steps])
    load_table.start()
    loads = []
    for step in range(steps):
        load = pltpu.make_async_copy(
            traces.at[:, pl.ds(step * span, span), :], buf.at[step], sems.at[step]
        )
        load.start()
        loads.append(load)
    lanes = lax.broadcasted_iota(jnp.int32, (1, 128), 1)
    bin4 = (FREQ_LO + lanes) % 4
    sign2 = jnp.where(bin4 % 2 == 0, 1.0, -1.0)
    direct = jnp.where(bin4 == 0, 1.0, jnp.where(bin4 == 2, -1.0, 0.0))
    up = jnp.where(bin4 == 1, 1.0, jnp.where(bin4 == 3, -1.0, 0.0))
    cross = jnp.where(lanes < 64, up, -up)
    lane32 = lanes // 32 % 2
    tiles = 2 * NBINS // 128

    def finish(step, dots):
        for start in range(0, span, ROWS):
            spans = []
            for w in range(windows):
                parts = []
                squares = jnp.zeros((ROWS, 128), jnp.float32)
                for t in range(tiles):
                    first_rows = [(q * windows + w) * span + start for q in range(QUARTERS)]
                    d0, d1, d2, d3 = (
                        dots[row : row + ROWS, t * 128 : (t + 1) * 128] for row in first_rows
                    )
                    main = d0 + sign2 * d2
                    turn = d1 + sign2 * d3
                    full = main + direct * turn + cross * pltpu.roll(turn, 64, 1)
                    squares = squares + full * full
                    parts.append(full)
                energy = jnp.sum(squares, axis=1, keepdims=True)
                scale = lax.rsqrt(energy / NBINS + EPS)
                spans.append([part * scale for part in parts])
            rows = pl.ds(step * span + start, ROWS)
            for t in range(tiles):
                first, second = spans[0][t], spans[1][t]
                even = jnp.where(lane32 == 0, first, pltpu.roll(second, 32, 1))
                odd = jnp.where(lane32 == 1, first, pltpu.roll(second, 96, 1))
                out[2 * t, rows] = even.astype(out.dtype)
                out[2 * t + 1, rows] = odd.astype(out.dtype)

    load_table.wait()
    before = None
    for step in range(steps):
        loads[step].wait()
        whole = buf[step].reshape(windows * span, length)
        stacked = jnp.concatenate(
            [whole[:, q * quarter : (q + 1) * quarter] for q in range(QUARTERS)], axis=0
        )
        dots = jnp.dot(stacked, table_buf[...], preferred_element_type=jnp.float32)
        if step:
            finish(step - 1, before)
        before = dots
    finish(steps - 1, before)


def in_hbm(values):
    return pltpu.with_memory_space_constraint(values, pltpu.HBM)


def whitened_groups(traces, steps=4):
    windows, channels, length = traces.shape
    table = jnp.asarray(packed_table(length))
    groups = NBINS // GROUP
    return pl.pallas_call(
        spectra_kernel,
        out_shape=jax.ShapeDtypeStruct((groups, channels, windows * 2 * GROUP), jnp.bfloat16),
        in_specs=[pl.BlockSpec(memory_space=pltpu.HBM), pl.BlockSpec(memory_space=pltpu.HBM)],
        out_specs=pl.BlockSpec(memory_space=pltpu.VMEM),
        scratch_shapes=[
            pltpu.VMEM(table.shape, table.dtype),
            pltpu.VMEM((steps, windows, channels // steps, length), traces.dtype),
            pltpu.SemaphoreType.DMA((steps + 1,)),
        ],
        compiler_params=pltpu.CompilerParams(vmem_limit_bytes=16 << 20),
        name="spectra",
    )(in_hbm(traces), in_hbm(table))


def products_kernel(groups, pairs, own, sib, *outs):
    lanes = lax.broadcasted_iota(jnp.int32, (BLOCK, 128), 1)
    is_re = lanes < 64
    dims = (((1,), (1,)), ((), ()))
    here_z = lax.axis_index("zh")
    here_y = lax.axis_index("y")
    core = lax.axis_index("core")
    cores = lax.axis_size("core")
    size_z = lax.axis_size("zh")
    size_y = lax.axis_size("y")
    for n, out in enumerate(outs):
        for i, e in enumerate(groups[n // size_y]):
            chip = (here_z + e) % size_z * size_y + (here_y + n % size_y) % size_y
            slot = chip * cores + core
            r = pairs[slot, 0]
            s = pairs[slot, 1]
            upper = []
            rotated = []
            lower = []
            for ref in (own, sib):
                block = ref[r]
                turned = pltpu.roll(block.astype(jnp.float32), 64, 1)
                upper.append(block)
                rotated.append(jnp.where(is_re, turned, -turned).astype(block.dtype))
                lower.append(ref[s])
            a = jnp.concatenate([jnp.concatenate(upper, 1), jnp.concatenate(rotated, 1)], 0)
            b = jnp.concatenate(lower, 1)
            both = lax.dot_general(a, b, dims, preferred_element_type=jnp.float32)
            out[i, 0] = both[:BLOCK].astype(out.dtype)
            out[i, 1] = both[BLOCK:].astype(out.dtype)


def vmem():
    return pl.BlockSpec(memory_space=pltpu.VMEM)


def partial_sums(groups, pairs, own, sib):
    size_y = lax.axis_size("y")
    outs = pl.pallas_call(
        functools.partial(products_kernel, groups),
        out_shape=[
            jax.ShapeDtypeStruct(
                (len(group), 2, BLOCK, BLOCK), jnp.bfloat16 if d else jnp.float32
            )
            for group in groups
            for d in range(size_y)
        ],
        in_specs=[pl.BlockSpec(memory_space=pltpu.SMEM), vmem(), vmem()],
        out_specs=[vmem()] * (len(groups) * size_y),
        compiler_params=pltpu.CompilerParams(vmem_limit_bytes=8 << 20),
        name="products",
    )(pairs, own, sib)
    return [outs[g * size_y : (g + 1) * size_y] for g in range(len(groups))]


def stage_kernel(*refs):
    came = refs[0].shape[0]
    for i in range(came):
        total = refs[0][i]
        for ref in refs[1:-came]:
            total = total + ref[i].astype(jnp.float32)
        out = refs[i - came]
        out[...] = total.astype(out.dtype)


def stage_sums(group, arrays):
    parts = len(group)
    shape = arrays[0].shape[1:]
    return pl.pallas_call(
        stage_kernel,
        out_shape=[jax.ShapeDtypeStruct(shape, jnp.bfloat16 if e else jnp.float32) for e in group],
        in_specs=[vmem()] * len(arrays),
        out_specs=[vmem()] * parts,
        compiler_params=pltpu.CompilerParams(vmem_limit_bytes=8 << 20),
        name="stage",
    )(*arrays)


def shifted(values, axis, offset):
    size = lax.axis_size(axis)
    return lax.ppermute(values, axis, [(i, (i + offset) % size) for i in range(size)])


def far_first(size):
    ways = [min(d, size - d) for d in range(size)]
    return [[d for d in range(size) if ways[d] == way] for way in sorted(set(ways), reverse=True)]


def spread(arrays, axis):
    order = [d for group in far_first(len(arrays)) for d in group if d]
    return [arrays[0]] + [shifted(arrays[d], axis, d) for d in order]


def on_device(traces, block_pairs, valid_count):
    windows = traces.shape[0] * lax.axis_size(("zh", "y", "core"))
    grouped = whitened_groups(traces)
    banded = lax.all_to_all(grouped, ("zl", "x"), split_axis=0, concat_axis=0, tiled=True)
    own = banded.reshape(-1, BLOCK, banded.shape[2])
    sib = shifted(own, "core", 1)
    parts = []
    first = None
    for group, arrays in zip(Z_GROUPS, partial_sums(Z_GROUPS, block_pairs, own, sib)):
        if first is not None:
            arrays, first = lax.optimization_barrier((arrays, first))
        along_y = spread(arrays, "y")
        first = along_y[1]
        staged = stage_sums(group, along_y)
        parts += [shifted(values, "zh", e) if e else values for e, values in zip(group, staged)]
    total = parts[0].astype(jnp.float32)
    for values in parts[1:]:
        total = total + values.astype(jnp.float32)
    stack_scale = 1.0 / math.sqrt(windows * GROUP)
    slot = lax.axis_index(("zh", "y", "core"))
    live = (slot < valid_count[0]).astype(jnp.float32)
    return (total * (stack_scale * live))[None, None]


def solution(mesh):
    fine = Mesh(mesh.devices.reshape(4, 4, 2, 2, 4), ("zh", "y", "core", "zl", "x"))
    win = ("zh", "y", "core")
    chan = ("zl", "x")
    return jax.shard_map(
        on_device,
        mesh=fine,
        in_specs=(P(win, chan, None), P(), P()),
        out_specs=P(win, chan, None, None, None),
        check_vma=False,
    )
```

```python
import functools
import math

import jax
import jax.numpy as jnp
import numpy as np
from jax import lax
from jax.experimental import pallas as pl
from jax.experimental.pallas import tpu as pltpu
from jax.sharding import Mesh, PartitionSpec as P

BLOCK = 128
NBINS = 256
FREQ_LO = 64
GROUP = 32
EPS = 1e-06
QUARTERS = 4
ROWS = 32
Z_GROUPS = ((2, 1), (3, 0))


def packed_table(length):
    times = np.arange(length // QUARTERS, dtype=np.int64)
    freqs = FREQ_LO + np.arange(NBINS, dtype=np.int64)
    angles = (times[:, None] * freqs[None, :] % length) * (2.0 * math.pi / length)
    factor = 1.0 / math.sqrt(length)
    re = (np.cos(angles) * factor).reshape(-1, NBINS // 64, 64)
    im = (-np.sin(angles) * factor).reshape(-1, NBINS // 64, 64)
    return np.concatenate([re, im], axis=2).reshape(-1, 2 * NBINS).astype(jnp.bfloat16)


def spectra_kernel(traces, table, out, table_buf, buf, sems):
    steps, windows, span, length = buf.shape
    quarter = length // QUARTERS
    load_table = pltpu.make_async_copy(table, table_buf, sems.at[steps])
    load_table.start()
    loads = []
    for step in range(steps):
        load = pltpu.make_async_copy(
            traces.at[:, pl.ds(step * span, span), :], buf.at[step], sems.at[step]
        )
        load.start()
        loads.append(load)
    lanes = lax.broadcasted_iota(jnp.int32, (1, 128), 1)
    bin4 = (FREQ_LO + lanes) % 4
    sign2 = jnp.where(bin4 % 2 == 0, 1.0, -1.0)
    direct = jnp.where(bin4 == 0, 1.0, jnp.where(bin4 == 2, -1.0, 0.0))
    up = jnp.where(bin4 == 1, 1.0, jnp.where(bin4 == 3, -1.0, 0.0))
    cross = jnp.where(lanes < 64, up, -up)
    lane32 = lanes // 32 % 2
    tiles = 2 * NBINS // 128

    def finish(step, dots):
        for start in range(0, span, ROWS):
            spans = []
            for w in range(windows):
                parts = []
                squares = jnp.zeros((ROWS, 128), jnp.float32)
                for t in range(tiles):
                    first_rows = [(q * windows + w) * span + start for q in range(QUARTERS)]
                    d0, d1, d2, d3 = (
                        dots[row : row + ROWS, t * 128 : (t + 1) * 128] for row in first_rows
                    )
                    main = d0 + sign2 * d2
                    turn = d1 + sign2 * d3
                    full = main + direct * turn + cross * pltpu.roll(turn, 64, 1)
                    squares = squares + full * full
                    parts.append(full)
                energy = jnp.sum(squares, axis=1, keepdims=True)
                scale = lax.rsqrt(energy / NBINS + EPS)
                spans.append([part * scale for part in parts])
            rows = pl.ds(step * span + start, ROWS)
            for t in range(tiles):
                first, second = spans[0][t], spans[1][t]
                even = jnp.where(lane32 == 0, first, pltpu.roll(second, 32, 1))
                odd = jnp.where(lane32 == 1, first, pltpu.roll(second, 96, 1))
                out[2 * t, rows] = even.astype(out.dtype)
                out[2 * t + 1, rows] = odd.astype(out.dtype)

    load_table.wait()
    before = None
    for step in range(steps):
        loads[step].wait()
        whole = buf[step].reshape(windows * span, length)
        stacked = jnp.concatenate(
            [whole[:, q * quarter : (q + 1) * quarter] for q in range(QUARTERS)], axis=0
        )
        dots = jnp.dot(stacked, table_buf[...], preferred_element_type=jnp.float32)
        if step:
            finish(step - 1, before)
        before = dots
    finish(steps - 1, before)


def in_hbm(values):
    return pltpu.with_memory_space_constraint(values, pltpu.HBM)


def whitened_groups(traces, steps=4):
    windows, channels, length = traces.shape
    table = jnp.asarray(packed_table(length))
    groups = NBINS // GROUP
    return pl.pallas_call(
        spectra_kernel,
        out_shape=jax.ShapeDtypeStruct((groups, channels, windows * 2 * GROUP), jnp.bfloat16),
        in_specs=[pl.BlockSpec(memory_space=pltpu.HBM), pl.BlockSpec(memory_space=pltpu.HBM)],
        out_specs=pl.BlockSpec(memory_space=pltpu.VMEM),
        scratch_shapes=[
            pltpu.VMEM(table.shape, table.dtype),
            pltpu.VMEM((steps, windows, channels // steps, length), traces.dtype),
            pltpu.SemaphoreType.DMA((steps + 1,)),
        ],
        compiler_params=pltpu.CompilerParams(vmem_limit_bytes=16 << 20),
        name="spectra",
    )(in_hbm(traces), in_hbm(table))


def products_kernel(groups, pairs, own, sib, *outs):
    lanes = lax.broadcasted_iota(jnp.int32, (BLOCK, 128), 1)
    is_re = lanes < 64
    dims = (((1,), (1,)), ((), ()))
    size_y = len(outs) // len(groups)
    for n, out in enumerate(outs):
        for i, e in enumerate(groups[n // size_y]):
            slot = e * size_y + n % size_y
            r = pairs[2 * slot]
            s = pairs[2 * slot + 1]
            upper = []
            rotated = []
            lower = []
            for ref in (own, sib):
                block = ref[r]
                turned = pltpu.roll(block.astype(jnp.float32), 64, 1)
                upper.append(block)
                rotated.append(jnp.where(is_re, turned, -turned).astype(block.dtype))
                lower.append(ref[s])
            a = jnp.concatenate([jnp.concatenate(upper, 1), jnp.concatenate(rotated, 1)], 0)
            b = jnp.concatenate(lower, 1)
            both = lax.dot_general(a, b, dims, preferred_element_type=jnp.float32)
            out[i, 0] = both[:BLOCK].astype(out.dtype)
            out[i, 1] = both[BLOCK:].astype(out.dtype)


def vmem():
    return pl.BlockSpec(memory_space=pltpu.VMEM)


def partial_sums(groups, pairs, own, sib):
    size_y = lax.axis_size("y")
    outs = pl.pallas_call(
        functools.partial(products_kernel, groups),
        out_shape=[
            jax.ShapeDtypeStruct(
                (len(group), 2, BLOCK, BLOCK), jnp.bfloat16 if d else jnp.float32
            )
            for group in groups
            for d in range(size_y)
        ],
        in_specs=[pl.BlockSpec(memory_space=pltpu.SMEM), vmem(), vmem()],
        out_specs=[vmem()] * (len(groups) * size_y),
        compiler_params=pltpu.CompilerParams(vmem_limit_bytes=8 << 20),
        name="products",
    )(pairs, own, sib)
    return [outs[g * size_y : (g + 1) * size_y] for g in range(len(groups))]


def stage_kernel(*refs):
    came = refs[0].shape[0]
    for i in range(came):
        total = refs[0][i]
        for ref in refs[1:-came]:
            total = total + ref[i].astype(jnp.float32)
        out = refs[i - came]
        out[...] = total.astype(out.dtype)


def stage_sums(group, arrays):
    parts = len(group)
    shape = arrays[0].shape[1:]
    return pl.pallas_call(
        stage_kernel,
        out_shape=[jax.ShapeDtypeStruct(shape, jnp.bfloat16 if e else jnp.float32) for e in group],
        in_specs=[vmem()] * len(arrays),
        out_specs=[vmem()] * parts,
        compiler_params=pltpu.CompilerParams(vmem_limit_bytes=8 << 20),
        name="stage",
    )(*arrays)


def shifted(values, axis, offset):
    size = lax.axis_size(axis)
    return lax.ppermute(values, axis, [(i, (i + offset) % size) for i in range(size)])


def near_first(size):
    return sorted(range(1, size), key=lambda d: min(d, size - d))


def spread(arrays, axis):
    return [arrays[0]] + [shifted(arrays[d], axis, d) for d in near_first(len(arrays))]


def pairs_by_distance(pairs):
    size_z = lax.axis_size("zh")
    size_y = lax.axis_size("y")
    table = pairs.reshape(size_z, size_y, lax.axis_size("core"), 2)
    table = jnp.concatenate([table, table], axis=0)
    table = jnp.concatenate([table, table], axis=1)
    start = (lax.axis_index("zh"), lax.axis_index("y"), lax.axis_index("core"), 0)
    return lax.dynamic_slice(table, start, (size_z, size_y, 1, 2)).reshape(-1)


def on_device(traces, block_pairs, valid_count):
    windows = traces.shape[0] * lax.axis_size(("zh", "y", "core"))
    grouped = whitened_groups(traces)
    banded = lax.all_to_all(grouped, ("zl", "x"), split_axis=0, concat_axis=0, tiled=True)
    own = banded.reshape(-1, BLOCK, banded.shape[2])
    sib = shifted(own, "core", 1)
    parts = []
    first = None
    for group, arrays in zip(Z_GROUPS, partial_sums(Z_GROUPS, pairs_by_distance(block_pairs), own, sib)):
        if first is not None:
            arrays, first = lax.optimization_barrier((arrays, first))
        along_y = spread(arrays, "y")
        first = along_y[1]
        staged = stage_sums(group, along_y)
        parts += [shifted(values, "zh", e) if e else values for e, values in zip(group, staged)]
    total = parts[0].astype(jnp.float32)
    for values in parts[1:]:
        total = total + values.astype(jnp.float32)
    stack_scale = 1.0 / math.sqrt(windows * GROUP)
    slot = lax.axis_index(("zh", "y", "core"))
    live = (slot < valid_count[0]).astype(jnp.float32)
    return (total * (stack_scale * live))[None, None]


def solution(mesh):
    fine = Mesh(mesh.devices.reshape(4, 4, 2, 2, 4), ("zh", "y", "core", "zl", "x"))
    win = ("zh", "y", "core")
    chan = ("zl", "x")
    return jax.shard_map(
        on_device,
        mesh=fine,
        in_specs=(P(win, chan, None), P(), P()),
        out_specs=P(win, chan, None, None, None),
        check_vma=False,
    )
```

```python
import functools
import math

import jax
import jax.numpy as jnp
import numpy as np
from jax import lax
from jax.experimental import pallas as pl
from jax.experimental.pallas import tpu as pltpu
from jax.sharding import Mesh, PartitionSpec as P

BLOCK = 128
NBINS = 256
FREQ_LO = 64
GROUP = 32
EPS = 1e-06
QUARTERS = 4
ROWS = 32
Z_GROUPS = ((1, 2), (3, 0))


def packed_table(length):
    times = np.arange(length // QUARTERS, dtype=np.int64)
    freqs = FREQ_LO + np.arange(NBINS, dtype=np.int64)
    angles = (times[:, None] * freqs[None, :] % length) * (2.0 * math.pi / length)
    factor = 1.0 / math.sqrt(length)
    re = (np.cos(angles) * factor).reshape(-1, NBINS // 64, 64)
    im = (-np.sin(angles) * factor).reshape(-1, NBINS // 64, 64)
    return np.concatenate([re, im], axis=2).reshape(-1, 2 * NBINS).astype(jnp.bfloat16)


def spectra_kernel(traces, table, out, table_buf, buf, sems):
    steps, windows, span, length = buf.shape
    quarter = length // QUARTERS
    load_table = pltpu.make_async_copy(table, table_buf, sems.at[steps])
    load_table.start()
    loads = []
    for step in range(steps):
        load = pltpu.make_async_copy(
            traces.at[:, pl.ds(step * span, span), :], buf.at[step], sems.at[step]
        )
        load.start()
        loads.append(load)
    lanes = lax.broadcasted_iota(jnp.int32, (1, 128), 1)
    bin4 = (FREQ_LO + lanes) % 4
    sign2 = jnp.where(bin4 % 2 == 0, 1.0, -1.0)
    direct = jnp.where(bin4 == 0, 1.0, jnp.where(bin4 == 2, -1.0, 0.0))
    up = jnp.where(bin4 == 1, 1.0, jnp.where(bin4 == 3, -1.0, 0.0))
    cross = jnp.where(lanes < 64, up, -up)
    lane32 = lanes // 32 % 2
    tiles = 2 * NBINS // 128

    def finish(step, dots):
        for start in range(0, span, ROWS):
            spans = []
            for w in range(windows):
                parts = []
                squares = jnp.zeros((ROWS, 128), jnp.float32)
                for t in range(tiles):
                    first_rows = [(q * windows + w) * span + start for q in range(QUARTERS)]
                    d0, d1, d2, d3 = (
                        dots[row : row + ROWS, t * 128 : (t + 1) * 128] for row in first_rows
                    )
                    main = d0 + sign2 * d2
                    turn = d1 + sign2 * d3
                    full = main + direct * turn + cross * pltpu.roll(turn, 64, 1)
                    squares = squares + full * full
                    parts.append(full)
                energy = jnp.sum(squares, axis=1, keepdims=True)
                scale = lax.rsqrt(energy / NBINS + EPS)
                spans.append([part * scale for part in parts])
            rows = pl.ds(step * span + start, ROWS)
            for t in range(tiles):
                first, second = spans[0][t], spans[1][t]
                even = jnp.where(lane32 == 0, first, pltpu.roll(second, 32, 1))
                odd = jnp.where(lane32 == 1, first, pltpu.roll(second, 96, 1))
                out[2 * t, rows] = even.astype(out.dtype)
                out[2 * t + 1, rows] = odd.astype(out.dtype)

    load_table.wait()
    before = None
    for step in range(steps):
        loads[step].wait()
        whole = buf[step].reshape(windows * span, length)
        stacked = jnp.concatenate(
            [whole[:, q * quarter : (q + 1) * quarter] for q in range(QUARTERS)], axis=0
        )
        dots = jnp.dot(stacked, table_buf[...], preferred_element_type=jnp.float32)
        if step:
            finish(step - 1, before)
        before = dots
    finish(steps - 1, before)


def in_hbm(values):
    return pltpu.with_memory_space_constraint(values, pltpu.HBM)


def whitened_groups(traces, steps=4):
    windows, channels, length = traces.shape
    table = jnp.asarray(packed_table(length))
    groups = NBINS // GROUP
    return pl.pallas_call(
        spectra_kernel,
        out_shape=jax.ShapeDtypeStruct((groups, channels, windows * 2 * GROUP), jnp.bfloat16),
        in_specs=[pl.BlockSpec(memory_space=pltpu.HBM), pl.BlockSpec(memory_space=pltpu.HBM)],
        out_specs=pl.BlockSpec(memory_space=pltpu.VMEM),
        scratch_shapes=[
            pltpu.VMEM(table.shape, table.dtype),
            pltpu.VMEM((steps, windows, channels // steps, length), traces.dtype),
            pltpu.SemaphoreType.DMA((steps + 1,)),
        ],
        compiler_params=pltpu.CompilerParams(vmem_limit_bytes=16 << 20),
        name="spectra",
    )(in_hbm(traces), in_hbm(table))


def products_kernel(groups, pairs, own, sib, *outs):
    lanes = lax.broadcasted_iota(jnp.int32, (BLOCK, 128), 1)
    is_re = lanes < 64
    dims = (((1,), (1,)), ((), ()))
    size_y = len(outs) // len(groups)
    for n, out in enumerate(outs):
        for i, e in enumerate(groups[n // size_y]):
            slot = e * size_y + n % size_y
            r = pairs[2 * slot]
            s = pairs[2 * slot + 1]
            upper = []
            rotated = []
            lower = []
            for ref in (own, sib):
                block = ref[r]
                turned = pltpu.roll(block.astype(jnp.float32), 64, 1)
                upper.append(block)
                rotated.append(jnp.where(is_re, turned, -turned).astype(block.dtype))
                lower.append(ref[s])
            a = jnp.concatenate([jnp.concatenate(upper, 1), jnp.concatenate(rotated, 1)], 0)
            b = jnp.concatenate(lower, 1)
            both = lax.dot_general(a, b, dims, preferred_element_type=jnp.float32)
            out[i, 0] = both[:BLOCK].astype(out.dtype)
            out[i, 1] = both[BLOCK:].astype(out.dtype)


def vmem():
    return pl.BlockSpec(memory_space=pltpu.VMEM)


def partial_sums(groups, pairs, own, sib):
    size_y = lax.axis_size("y")
    outs = pl.pallas_call(
        functools.partial(products_kernel, groups),
        out_shape=[
            jax.ShapeDtypeStruct(
                (len(group), 2, BLOCK, BLOCK), jnp.bfloat16 if d else jnp.float32
            )
            for group in groups
            for d in range(size_y)
        ],
        in_specs=[pl.BlockSpec(memory_space=pltpu.SMEM), vmem(), vmem()],
        out_specs=[vmem()] * (len(groups) * size_y),
        compiler_params=pltpu.CompilerParams(vmem_limit_bytes=8 << 20),
        name="products",
    )(pairs, own, sib)
    return [outs[g * size_y : (g + 1) * size_y] for g in range(len(groups))]


def stage_kernel(*refs):
    came = refs[0].shape[0]
    for i in range(came):
        total = refs[0][i]
        for ref in refs[1:-came]:
            total = total + ref[i].astype(jnp.float32)
        out = refs[i - came]
        out[...] = total.astype(out.dtype)


def stage_sums(group, arrays):
    parts = len(group)
    shape = arrays[0].shape[1:]
    return pl.pallas_call(
        stage_kernel,
        out_shape=[jax.ShapeDtypeStruct(shape, jnp.bfloat16 if e else jnp.float32) for e in group],
        in_specs=[vmem()] * len(arrays),
        out_specs=[vmem()] * parts,
        compiler_params=pltpu.CompilerParams(vmem_limit_bytes=8 << 20),
        name="stage",
    )(*arrays)


def shifted(values, axis, offset):
    size = lax.axis_size(axis)
    return lax.ppermute(values, axis, [(i, (i + offset) % size) for i in range(size)])


def near_first(size):
    return sorted(range(1, size), key=lambda d: min(d, size - d))


def spread(arrays, axis):
    return [arrays[0]] + [shifted(arrays[d], axis, d) for d in near_first(len(arrays))]


def pairs_by_distance(pairs):
    size_z = lax.axis_size("zh")
    size_y = lax.axis_size("y")
    table = pairs.reshape(size_z, size_y, lax.axis_size("core"), 2)
    table = jnp.concatenate([table, table], axis=0)
    table = jnp.concatenate([table, table], axis=1)
    start = (lax.axis_index("zh"), lax.axis_index("y"), lax.axis_index("core"), 0)
    return lax.dynamic_slice(table, start, (size_z, size_y, 1, 2)).reshape(-1)


def on_device(traces, block_pairs, valid_count):
    windows = traces.shape[0] * lax.axis_size(("zh", "y", "core"))
    grouped = whitened_groups(traces)
    banded = lax.all_to_all(grouped, ("zl", "x"), split_axis=0, concat_axis=0, tiled=True)
    own = banded.reshape(-1, BLOCK, banded.shape[2])
    sib = shifted(own, "core", 1)
    parts = []
    sums = partial_sums(Z_GROUPS, pairs_by_distance(block_pairs), own, sib)
    for group, arrays in zip(Z_GROUPS, sums):
        along_y = spread(arrays, "y")
        staged = stage_sums(group, along_y)
        parts += [shifted(values, "zh", e) if e else values for e, values in zip(group, staged)]
    total = parts[0].astype(jnp.float32)
    for values in parts[1:]:
        total = total + values.astype(jnp.float32)
    stack_scale = 1.0 / math.sqrt(windows * GROUP)
    slot = lax.axis_index(("zh", "y", "core"))
    live = (slot < valid_count[0]).astype(jnp.float32)
    return (total * (stack_scale * live))[None, None]


def solution(mesh):
    fine = Mesh(mesh.devices.reshape(4, 4, 2, 2, 4), ("zh", "y", "core", "zl", "x"))
    win = ("zh", "y", "core")
    chan = ("zl", "x")
    return jax.shard_map(
        on_device,
        mesh=fine,
        in_specs=(P(win, chan, None), P(), P()),
        out_specs=P(win, chan, None, None, None),
        check_vma=False,
    )
```

```python
import functools
import math

import jax
import jax.numpy as jnp
import numpy as np
from jax import lax
from jax.experimental import pallas as pl
from jax.experimental.pallas import tpu as pltpu
from jax.sharding import Mesh, PartitionSpec as P

BLOCK = 128
NBINS = 256
FREQ_LO = 64
GROUP = 32
EPS = 1e-06
QUARTERS = 4
ROWS = 32
CHUNKS = (0, 64, 160, 256)
Z_GROUPS = ((2, 1), (3, 0))


def packed_table(length):
    times = np.arange(length // QUARTERS, dtype=np.int64)
    freqs = FREQ_LO + np.arange(NBINS, dtype=np.int64)
    angles = (times[:, None] * freqs[None, :] % length) * (2.0 * math.pi / length)
    factor = 1.0 / math.sqrt(length)
    re = (np.cos(angles) * factor).reshape(-1, NBINS // 64, 64)
    im = (-np.sin(angles) * factor).reshape(-1, NBINS // 64, 64)
    return np.concatenate([re, im], axis=2).reshape(-1, 2 * NBINS).astype(jnp.bfloat16)


def spectra_kernel(traces, table, out, table_buf, buf, sems):
    windows, _, length = buf.shape
    quarter = length // QUARTERS
    steps = len(CHUNKS) - 1
    load_table = pltpu.make_async_copy(table, table_buf, sems.at[steps])
    load_table.start()
    loads = []
    for step in range(steps):
        chunk = pl.ds(CHUNKS[step], CHUNKS[step + 1] - CHUNKS[step])
        load = pltpu.make_async_copy(traces.at[:, chunk], buf.at[:, chunk], sems.at[step])
        load.start()
        loads.append(load)
    lanes = lax.broadcasted_iota(jnp.int32, (1, 128), 1)
    bin4 = (FREQ_LO + lanes) % 4
    sign2 = jnp.where(bin4 % 2 == 0, 1.0, -1.0)
    direct = jnp.where(bin4 == 0, 1.0, jnp.where(bin4 == 2, -1.0, 0.0))
    up = jnp.where(bin4 == 1, 1.0, jnp.where(bin4 == 3, -1.0, 0.0))
    cross = jnp.where(lanes < 64, up, -up)
    lane32 = lanes // 32 % 2
    tiles = 2 * NBINS // 128

    def finish(step, dots):
        span = CHUNKS[step + 1] - CHUNKS[step]
        for start in range(0, span, ROWS):
            spans = []
            for w in range(windows):
                parts = []
                squares = jnp.zeros((ROWS, 128), jnp.float32)
                for t in range(tiles):
                    first_rows = [(q * windows + w) * span + start for q in range(QUARTERS)]
                    d0, d1, d2, d3 = (
                        dots[row : row + ROWS, t * 128 : (t + 1) * 128] for row in first_rows
                    )
                    main = d0 + sign2 * d2
                    turn = d1 + sign2 * d3
                    full = main + direct * turn + cross * pltpu.roll(turn, 64, 1)
                    squares = squares + full * full
                    parts.append(full)
                energy = jnp.sum(squares, axis=1, keepdims=True)
                scale = lax.rsqrt(energy / NBINS + EPS)
                spans.append([part * scale for part in parts])
            rows = pl.ds(CHUNKS[step] + start, ROWS)
            for t in range(tiles):
                first, second = spans[0][t], spans[1][t]
                even = jnp.where(lane32 == 0, first, pltpu.roll(second, 32, 1))
                odd = jnp.where(lane32 == 1, first, pltpu.roll(second, 96, 1))
                out[2 * t, rows] = even.astype(out.dtype)
                out[2 * t + 1, rows] = odd.astype(out.dtype)

    load_table.wait()
    before = None
    for step in range(steps):
        loads[step].wait()
        whole = buf[:, CHUNKS[step] : CHUNKS[step + 1]].reshape(-1, length)
        stacked = jnp.concatenate(
            [whole[:, q * quarter : (q + 1) * quarter] for q in range(QUARTERS)], axis=0
        )
        dots = jnp.dot(stacked, table_buf[...], preferred_element_type=jnp.float32)
        if step:
            finish(step - 1, before)
        before = dots
    finish(steps - 1, before)


def in_hbm(values):
    return pltpu.with_memory_space_constraint(values, pltpu.HBM)


def whitened_groups(traces):
    windows, channels, length = traces.shape
    table = jnp.asarray(packed_table(length))
    groups = NBINS // GROUP
    return pl.pallas_call(
        spectra_kernel,
        out_shape=jax.ShapeDtypeStruct((groups, channels, windows * 2 * GROUP), jnp.bfloat16),
        in_specs=[pl.BlockSpec(memory_space=pltpu.HBM), pl.BlockSpec(memory_space=pltpu.HBM)],
        out_specs=pl.BlockSpec(memory_space=pltpu.VMEM),
        scratch_shapes=[
            pltpu.VMEM(table.shape, table.dtype),
            pltpu.VMEM(traces.shape, traces.dtype),
            pltpu.SemaphoreType.DMA((len(CHUNKS),)),
        ],
        compiler_params=pltpu.CompilerParams(vmem_limit_bytes=16 << 20),
        name="spectra",
    )(in_hbm(traces), in_hbm(table))


def products_kernel(groups, pairs, own, sib, *outs):
    lanes = lax.broadcasted_iota(jnp.int32, (BLOCK, 128), 1)
    is_re = lanes < 64
    dims = (((1,), (1,)), ((), ()))
    size_y = len(outs) // len(groups)
    for n, out in enumerate(outs):
        for i, e in enumerate(groups[n // size_y]):
            slot = e * size_y + n % size_y
            r = pairs[2 * slot]
            s = pairs[2 * slot + 1]
            upper = []
            rotated = []
            lower = []
            for ref in (own, sib):
                block = ref[r]
                turned = pltpu.roll(block.astype(jnp.float32), 64, 1)
                upper.append(block)
                rotated.append(jnp.where(is_re, turned, -turned).astype(block.dtype))
                lower.append(ref[s])
            a = jnp.concatenate([jnp.concatenate(upper, 1), jnp.concatenate(rotated, 1)], 0)
            b = jnp.concatenate(lower, 1)
            both = lax.dot_general(a, b, dims, preferred_element_type=jnp.float32)
            out[i, 0] = both[:BLOCK].astype(out.dtype)
            out[i, 1] = both[BLOCK:].astype(out.dtype)


def vmem():
    return pl.BlockSpec(memory_space=pltpu.VMEM)


def partial_sums(groups, pairs, own, sib):
    size_y = lax.axis_size("y")
    outs = pl.pallas_call(
        functools.partial(products_kernel, groups),
        out_shape=[
            jax.ShapeDtypeStruct(
                (len(group), 2, BLOCK, BLOCK), jnp.bfloat16 if d else jnp.float32
            )
            for group in groups
            for d in range(size_y)
        ],
        in_specs=[pl.BlockSpec(memory_space=pltpu.SMEM), vmem(), vmem()],
        out_specs=[vmem()] * (len(groups) * size_y),
        compiler_params=pltpu.CompilerParams(vmem_limit_bytes=8 << 20),
        name="products",
    )(pairs, own, sib)
    return [outs[g * size_y : (g + 1) * size_y] for g in range(len(groups))]


def stage_kernel(*refs):
    came = refs[0].shape[0]
    for i in range(came):
        total = refs[0][i]
        for ref in refs[1:-came]:
            total = total + ref[i].astype(jnp.float32)
        out = refs[i - came]
        out[...] = total.astype(out.dtype)


def stage_sums(group, arrays):
    parts = len(group)
    shape = arrays[0].shape[1:]
    return pl.pallas_call(
        stage_kernel,
        out_shape=[jax.ShapeDtypeStruct(shape, jnp.bfloat16 if e else jnp.float32) for e in group],
        in_specs=[vmem()] * len(arrays),
        out_specs=[vmem()] * parts,
        compiler_params=pltpu.CompilerParams(vmem_limit_bytes=8 << 20),
        name="stage",
    )(*arrays)


def shifted(values, axis, offset):
    size = lax.axis_size(axis)
    return lax.ppermute(values, axis, [(i, (i + offset) % size) for i in range(size)])


def near_first(size):
    return sorted(range(1, size), key=lambda d: min(d, size - d))


def spread(arrays, axis):
    return [arrays[0]] + [shifted(arrays[d], axis, d) for d in near_first(len(arrays))]


def pairs_by_distance(pairs):
    size_z = lax.axis_size("zh")
    size_y = lax.axis_size("y")
    table = pairs.reshape(size_z, size_y, lax.axis_size("core"), 2)
    table = jnp.concatenate([table, table], axis=0)
    table = jnp.concatenate([table, table], axis=1)
    start = (lax.axis_index("zh"), lax.axis_index("y"), lax.axis_index("core"), 0)
    return lax.dynamic_slice(table, start, (size_z, size_y, 1, 2)).reshape(-1)


def on_device(traces, block_pairs, valid_count):
    windows = traces.shape[0] * lax.axis_size(("zh", "y", "core"))
    grouped = whitened_groups(traces)
    banded = lax.all_to_all(grouped, ("zl", "x"), split_axis=0, concat_axis=0, tiled=True)
    own = banded.reshape(-1, BLOCK, banded.shape[2])
    sib = shifted(own, "core", 1)
    parts = []
    first = None
    for group, arrays in zip(Z_GROUPS, partial_sums(Z_GROUPS, pairs_by_distance(block_pairs), own, sib)):
        if first is not None:
            arrays, first = lax.optimization_barrier((arrays, first))
        along_y = spread(arrays, "y")
        first = along_y[1]
        staged = stage_sums(group, along_y)
        parts += [shifted(values, "zh", e) if e else values for e, values in zip(group, staged)]
    total = parts[0].astype(jnp.float32)
    for values in parts[1:]:
        total = total + values.astype(jnp.float32)
    stack_scale = 1.0 / math.sqrt(windows * GROUP)
    slot = lax.axis_index(("zh", "y", "core"))
    live = (slot < valid_count[0]).astype(jnp.float32)
    return (total * (stack_scale * live))[None, None]


def solution(mesh):
    fine = Mesh(mesh.devices.reshape(4, 4, 2, 2, 4), ("zh", "y", "core", "zl", "x"))
    win = ("zh", "y", "core")
    chan = ("zl", "x")
    return jax.shard_map(
        on_device,
        mesh=fine,
        in_specs=(P(win, chan, None), P(), P()),
        out_specs=P(win, chan, None, None, None),
        check_vma=False,
    )
```
